128 devices in a mesh: row: 8 (over y, core), col: 16 (over x, z).
Axes of the slice: x: 4, y: 4, z: 4, core: 2. Of those that a mesh axis runs over, the one named last changes fastest.
Arguments:
- x_slots: bfloat16 [8, 16, 128, 128, 128], P('row', 'col'), may hold values from -0.875 to 0.875
- block_pairs: int32 [8, 16], replicated, may hold values from -1 to 15, as said below
- greens: bfloat16 [2, 512, 512], replicated, may hold values from -0.25 to 0.25
- green_mask: int32 [2, 4, 4], replicated, may hold values 0 or 1
- chi_mask: int32 [8, 8], P('row'), may hold values 0 or 1
Outputs:
- chi_blocks: float32 [1024, 1024], P(('row', 'col'))
The draws below stay inside these ranges and needn't reach their ends.
Inputs may be any that keep to these rules, and one draw needn't show every extreme that they name: `block_pairs`: in each row exactly 10 slots name basis-pair blocks, all different, and all other slots are -1; in every row, all 1 slots of some col index are named.
All inputs are finite; a program needn't handle non-finite values. No bound on the sum of `chi_mask` on one device may be relied on, other than what follows from the above.
Results may differ from the reference program's by a relative error of at most 0.0041.
Values may be sent and summed in bfloat16 or wider, within the bound.
No kernel may reach another device: no remote copies, remote signals or barrier semaphores. Data moves between devices by JAX's collectives and lax.ppermute only.
A program may use at most 64 MiB of HBM per device.

```python
import jax
import jax.numpy as jnp
from jax import lax

B = 128
AB = 128
NBLK = 4
NBAS = 512
NAUX = 1024
NNZ = 10
SLOTS = 1
N_ROW = 8
N_COL = 16


def draw_block_pairs(key, part):
    row_keys = jax.random.split(key, N_ROW)

    def one_row(row_key):
        first_key, second_key, third_key = jax.random.split(row_key, 3)
        total = N_COL * SLOTS
        filled_owner = jax.random.randint(first_key, (), 0, N_COL)
        priority = jax.random.permutation(second_key, total).astype(jnp.int32)
        owner = jnp.arange(total, dtype=jnp.int32) // SLOTS
        score = jnp.where(owner == filled_owner, priority - total, priority)
        order = jnp.argsort(score, stable=True)
        placing = jnp.argsort(order, stable=True).astype(jnp.int32)
        shuffled = jax.random.permutation(third_key, NBLK * NBLK).astype(jnp.int32)
        picked = shuffled[jnp.minimum(placing, NBLK * NBLK - 1)]
        return jnp.where(placing < NNZ, picked, -1).astype(jnp.int32)
    return jax.vmap(one_row)(row_keys)


def touch_ends(result, own_key, smallest, largest):
    index_at = [jax.random.randint(jax.random.fold_in(own_key, axis), (), 0, length) for axis, length in enumerate(result.shape)]
    widest = result.shape.index(max(result.shape))
    neighbour = index_at[:widest] + [(index_at[widest] + 1) % result.shape[widest]] + index_at[widest + 1:]
    return result.at[tuple(index_at)].set(smallest).at[tuple(neighbour)].set(largest)


def steps_of(own_key, extent, shards, least, top_value):
    level, own = 1.0, jax.random.fold_in(own_key, 6)
    for axis_at, blocks in shards:
        draws = jnp.exp(jax.random.uniform(jax.random.fold_in(own, axis_at), (blocks,), jnp.float32, least / len(shards), top_value / len(shards)))
        level = level * jnp.repeat(draws, extent[axis_at] // blocks).reshape([-1 if axis == axis_at else 1 for axis in range(len(extent))])
    return level


def centred(rng, shape, scale, bound, pieces=(), kind=jnp.bfloat16):
    values = jax.random.normal(rng, shape, jnp.float32) * scale
    if len(pieces) > 0:
        values = steps_of(rng, shape, pieces, -0.22, 0.18) * values
    return jnp.clip(values, min=-bound, max=bound).astype(kind)


def setup_inputs(seed: int = 0) -> dict:
    seeds = jax.random.split(jax.random.key(seed), 6)
    x_slots = centred(seeds[0], (N_ROW, N_COL * SLOTS, AB, B, B), (1.4 / (NBLK * B) ** 0.5), 0.875, ((0, 8), (1, 16)))
    block_pairs = draw_block_pairs(jax.random.fold_in(seeds[5], 71), 0)
    greens = centred(seeds[2], (2, NBAS, NBAS), NBAS ** -0.5, 0.25)
    green_mask = touch_ends((jax.random.randint(seeds[3], (2, NBLK, NBLK), 0, 4) < 3).astype(jnp.int32), jax.random.fold_in(seeds[3], 1), 0, 1)
    chi_mask = touch_ends((jax.random.randint(seeds[4], (N_ROW, N_ROW), 0, 4) < 3).astype(jnp.int32), jax.random.fold_in(seeds[4], 1), 0, 1)
    return dict(x_slots=x_slots, block_pairs=block_pairs, greens=greens, green_mask=green_mask, chi_mask=chi_mask)


def assemble(stored, pair_list):
    selector = (pair_list[:, None] == jnp.arange(NBLK * NBLK, dtype=jnp.int32)[None, :]).astype(jnp.float32)
    pair_blocks = jnp.einsum('kq,kabc->qabc', selector, stored.astype(jnp.float32))
    pair_blocks = pair_blocks.reshape(NBLK, NBLK, AB, B, B).transpose(2, 0, 3, 1, 4)
    return pair_blocks.reshape(AB, NBLK * B, NBLK * B).astype(jnp.bfloat16)


def reference(x_slots, block_pairs, greens, green_mask, chi_mask):
    basis_count = NBLK * B
    full_mask = jnp.repeat(jnp.repeat(green_mask, B, axis=1), B, axis=2).astype(jnp.bfloat16)
    masked = greens * full_mask
    occupied = masked[0].astype(jnp.float32)
    virtual = masked[1].astype(jnp.float32)

    def one_group(operands):
        stored, pair_list = operands
        dense_x = assemble(stored, pair_list)
        half_done = jnp.einsum('ml,pmn->pln', occupied, dense_x.astype(jnp.float32)).astype(jnp.bfloat16)
        contracted = jnp.einsum('pln,ns->pls', half_done.astype(jnp.float32), virtual).astype(jnp.bfloat16)
        return contracted.reshape(AB, basis_count * basis_count), dense_x.reshape(AB, basis_count * basis_count)

    contracted_all, dense_all = lax.map(one_group, (x_slots, block_pairs))
    contracted_all = contracted_all.reshape(NAUX, basis_count * basis_count)
    dense_all = dense_all.reshape(NAUX, basis_count * basis_count)
    chi_sum = lax.dot_general(contracted_all, dense_all, (((1,), (1,)), ((), ())), preferred_element_type=jnp.float32)
    keep = jnp.repeat(jnp.repeat(chi_mask, AB, axis=0), AB, axis=1).astype(jnp.float32)
    return chi_sum * keep
```

```python
import jax
import jax.numpy as jnp
from jax import lax
from jax.experimental import pallas as pl
from jax.experimental.pallas import tpu as pltpu
from jax.sharding import Mesh
from jax.sharding import PartitionSpec as P

B = 128
AB = 128
NBLK = 4
NPAIR = NBLK * NBLK
NBAS = NBLK * B
NNZ = 10
N_ROW = 8
N_COL = 16
AUX = AB // N_COL
NCHIP = 64
SUB = B // NCHIP
SPAN = SUB * B
ROWS = NCHIP * AUX
VMEM_LIMIT = 60 * 1024 * 1024


def named_kernel(slot_of_ref, arrived_ref, out_ref, scratch):
    for aux in range(AUX):
        for j in range(NNZ):
            block = arrived_ref[slot_of_ref[j], aux].astype(jnp.float32)
            for sub in range(SUB):
                scratch[j * SUB + sub, pl.ds(aux, NCHIP, stride=AUX), :] = block[
                    sub * NCHIP : (sub + 1) * NCHIP
                ]
    for k in range(NNZ * SUB):
        out_ref[:, k * B : (k + 1) * B] = scratch[k].astype(jnp.bfloat16)


def named_slices(slot_of, arrived):
    return pl.pallas_call(
        named_kernel,
        out_shape=jax.ShapeDtypeStruct((ROWS, NNZ * SPAN), jnp.bfloat16),
        grid_spec=pltpu.PrefetchScalarGridSpec(
            num_scalar_prefetch=1,
            grid=(),
            in_specs=[pl.BlockSpec(memory_space=pltpu.VMEM)],
            out_specs=pl.BlockSpec(memory_space=pltpu.VMEM),
            scratch_shapes=[pltpu.VMEM((NNZ * SUB, ROWS, B), jnp.float32)],
        ),
        compiler_params=pltpu.CompilerParams(vmem_limit_bytes=VMEM_LIMIT),
        name="named_slices",
    )(slot_of, arrived)


def contract_kernel(block_slot_ref, arrived_ref, occ_t_ref, virt_ref, out_ref, scratch, dense):
    def one(aux, carry):
        for m in range(NBLK):
            for n in range(NBLK):
                slot = block_slot_ref[m * NBLK + n]
                block = arrived_ref[jnp.maximum(slot, 0), aux]
                keep = jnp.where(slot >= 0, 1.0, 0.0)
                block = jnp.where(keep > 0.5, block.astype(jnp.float32), 0.0).astype(jnp.bfloat16)
                dense[m * B : (m + 1) * B, n * B : (n + 1) * B] = block
        half = jnp.dot(
            occ_t_ref[...], dense[...], preferred_element_type=jnp.float32
        ).astype(jnp.bfloat16)
        full = jnp.dot(half, virt_ref[...], preferred_element_type=jnp.float32)
        for m in range(NBLK):
            for sub in range(SUB):
                row = m * B + sub * NCHIP
                for n in range(NBLK):
                    scratch[(m * NBLK + n) * SUB + sub, pl.ds(aux, NCHIP, stride=AUX), :] = full[
                        row : row + NCHIP, n * B : (n + 1) * B
                    ]
        return carry

    lax.fori_loop(0, AUX, one, 0)
    for k in range(NPAIR * SUB):
        out_ref[:, k * B : (k + 1) * B] = scratch[k].astype(jnp.bfloat16)


def contracted_slices(block_slot, arrived, occ_t, virt):
    return pl.pallas_call(
        contract_kernel,
        out_shape=jax.ShapeDtypeStruct((ROWS, NPAIR * SPAN), jnp.bfloat16),
        grid_spec=pltpu.PrefetchScalarGridSpec(
            num_scalar_prefetch=1,
            grid=(),
            in_specs=[pl.BlockSpec(memory_space=pltpu.VMEM)] * 3,
            out_specs=pl.BlockSpec(memory_space=pltpu.VMEM),
            scratch_shapes=[
                pltpu.VMEM((NPAIR * SUB, ROWS, B), jnp.float32),
                pltpu.VMEM((NBAS, NBAS), jnp.bfloat16),
            ],
        ),
        compiler_params=pltpu.CompilerParams(vmem_limit_bytes=VMEM_LIMIT),
        name="contracted_slices",
    )(block_slot, arrived, occ_t, virt)


def chi_kernel(pairs_ref, core_ref, image_ref, own_ref, other_ref, out_ref):
    core = core_ref[0]
    for y in range(N_ROW // 2):
        for ref, side in ((own_ref, core), (other_ref, 1 - core)):
            row = 2 * y + side
            total = jnp.zeros((ROWS, AB), jnp.float32)
            for j in range(NNZ):
                start = pl.multiple_of(pairs_ref[row, j] * SPAN, SPAN)
                total += lax.dot_general(
                    image_ref[:, pl.ds(start, SPAN)],
                    ref[y * AB : (y + 1) * AB, j * SPAN : (j + 1) * SPAN],
                    (((1,), (1,)), ((), ())),
                    preferred_element_type=jnp.float32,
                )
            out_ref[:, pl.ds(pl.multiple_of(row * AB, AB), AB)] = total.astype(jnp.bfloat16)


def chi_partials(pairs, core, image, own, other):
    return pl.pallas_call(
        chi_kernel,
        out_shape=jax.ShapeDtypeStruct((ROWS, N_ROW * AB), jnp.bfloat16),
        grid_spec=pltpu.PrefetchScalarGridSpec(
            num_scalar_prefetch=2,
            grid=(),
            in_specs=[pl.BlockSpec(memory_space=pltpu.VMEM)] * 3,
            out_specs=pl.BlockSpec(memory_space=pltpu.VMEM),
        ),
        compiler_params=pltpu.CompilerParams(vmem_limit_bytes=VMEM_LIMIT),
        name="chi_partials",
    )(pairs, core, image, own, other)


def on_device(x_slots, block_pairs, greens, green_mask, chi_mask):
    core = lax.axis_index("c").astype(jnp.int32)
    row = lax.axis_index(("y", "c"))
    chips = ("y", "x", "z")
    named = (block_pairs >= 0).astype(jnp.int32)
    place = jnp.cumsum(named, axis=1) - 1
    hit = (place[:, None, :] == jnp.arange(NNZ)[None, :, None]) & (named[:, None, :] > 0)
    pairs = jnp.sum(jnp.where(hit, block_pairs[:, None, :], 0), axis=2)
    own_hit = lax.dynamic_index_in_dim(hit, row, 0, keepdims=False)
    slot_ids = jnp.arange(N_COL, dtype=jnp.int32)
    slot_of = jnp.sum(jnp.where(own_hit, slot_ids[None, :], 0), axis=1)
    own_pairs = lax.dynamic_index_in_dim(block_pairs, row, 0, keepdims=False)
    at_block = own_pairs[None, :] == jnp.arange(NPAIR, dtype=jnp.int32)[:, None]
    block_slot = jnp.sum(jnp.where(at_block, slot_ids[None, :] + 1, 0), axis=1) - 1

    masked = greens.reshape(2, NBLK, B, NBLK, B) * green_mask.astype(jnp.bfloat16)[
        :, :, None, :, None
    ]
    masked = masked.reshape(2, NBAS, NBAS)
    occ_t = masked[0].T
    virt = masked[1]

    arrived = lax.all_to_all(
        x_slots[0, 0].reshape(N_COL, AUX, B, B), ("x", "z"), 0, 0, tiled=True
    )
    own = named_slices(slot_of, arrived)
    own = lax.all_to_all(
        own.reshape(NCHIP, AUX, NNZ * SPAN), chips, 0, 0, tiled=True
    ).reshape(ROWS, NNZ * SPAN)
    other = lax.ppermute(own, "c", [(0, 1), (1, 0)])
    image = contracted_slices(block_slot, arrived, occ_t, virt)
    image = lax.all_to_all(
        image.reshape(NCHIP, AUX, NPAIR * SPAN), chips, 0, 0, tiled=True
    ).reshape(ROWS, NPAIR * SPAN)
    part = chi_partials(pairs, core[None], image, own, other)
    part = lax.all_to_all(part.reshape(NCHIP, AUX, N_ROW * AB), chips, 0, 0, tiled=True)
    chi = jnp.sum(part.astype(jnp.float32), axis=0)
    return chi * jnp.repeat(chi_mask[0], AB).astype(jnp.float32)[None, :]


def solution(mesh):
    split = Mesh(mesh.devices.reshape(4, 2, 4, 4), ("y", "c", "x", "z"))
    row, col = ("y", "c"), ("x", "z")
    placed = (P(row, col, None, None, None), P(), P(), P(), P(row, None))
    return jax.shard_map(
        on_device,
        mesh=split,
        in_specs=placed,
        out_specs=P(row + col, None),
        check_vma=False,
    )
```

```python
import jax
import jax.numpy as jnp
from jax import lax
from jax.experimental import pallas as pl
from jax.experimental.pallas import tpu as pltpu
from jax.sharding import Mesh
from jax.sharding import PartitionSpec as P

B = 128
AB = 128
NBLK = 4
NPAIR = NBLK * NBLK
NBAS = NBLK * B
NNZ = 10
N_ROW = 8
N_COL = 16
AUX = AB // N_COL
NCHIP = 64
SUB = B // NCHIP
SPAN = SUB * B
ROWS = NCHIP * AUX
MIB = 1024 * 1024
SMEM = pl.BlockSpec(memory_space=pltpu.SMEM)
VMEM = pl.BlockSpec(memory_space=pltpu.VMEM)
HBM = pl.BlockSpec(memory_space=pltpu.HBM)


def named_kernel(
    block_pairs_ref, arrived_ref, out_ref, slot_of_ref, blocks, scratch, rows_ref, in_sem, out_sem
):
    row = lax.axis_index(("y", "c")).astype(jnp.int32)
    place = jnp.int32(0)
    for k in range(N_COL):
        slot_of_ref[place] = k
        place = jnp.minimum(place + (block_pairs_ref[row, k] >= 0).astype(jnp.int32), N_COL - 1)
    reads, writes = [], []
    for j in range(NNZ):
        reads.append(
            pltpu.make_async_copy(arrived_ref.at[slot_of_ref[j]], blocks.at[j], in_sem.at[j])
        )
        reads[-1].start()
    for j in range(NNZ):
        reads[j].wait()
        for aux in range(AUX):
            block = blocks[j, aux].astype(jnp.float32)
            for sub in range(SUB):
                scratch[j % 2, sub, pl.ds(aux, NCHIP, stride=AUX), :] = block[
                    sub * NCHIP : (sub + 1) * NCHIP
                ]
        for sub in range(SUB):
            rows_ref[:, j * SPAN + sub * B : j * SPAN + (sub + 1) * B] = scratch[
                j % 2, sub
            ].astype(jnp.bfloat16)
        cols = pl.ds(j * SPAN, SPAN)
        writes.append(
            pltpu.make_async_copy(rows_ref.at[:, cols], out_ref.at[:, cols], out_sem.at[j])
        )
        writes[-1].start()
    for copy in writes:
        copy.wait()


def named_slices(block_pairs, arrived):
    return pl.pallas_call(
        named_kernel,
        out_shape=jax.ShapeDtypeStruct((ROWS, NNZ * SPAN), jnp.bfloat16),
        grid_spec=pltpu.PrefetchScalarGridSpec(
            num_scalar_prefetch=1,
            grid=(),
            in_specs=[HBM],
            out_specs=HBM,
            scratch_shapes=[
                pltpu.SMEM((N_COL,), jnp.int32),
                pltpu.VMEM((NNZ, AUX, B, B), jnp.bfloat16),
                pltpu.VMEM((2, SUB, ROWS, B), jnp.float32),
                pltpu.VMEM((ROWS, NNZ * SPAN), jnp.bfloat16),
                pltpu.SemaphoreType.DMA((NNZ,)),
                pltpu.SemaphoreType.DMA((NNZ,)),
            ],
        ),
        compiler_params=pltpu.CompilerParams(vmem_limit_bytes=62 * MIB),
        name="named_slices",
    )(block_pairs, arrived)


def contract_kernel(
    block_pairs_ref,
    mask_ref,
    arrived_ref,
    greens_ref,
    out_ref,
    scratch,
    dense,
    occ_t_ref,
    virt_ref,
    block_slot_ref,
):
    for pair in range(NPAIR):
        block_slot_ref[pair] = -1
    row = lax.axis_index(("y", "c")).astype(jnp.int32)
    for k in range(N_COL):
        pair = block_pairs_ref[row, k]

        @pl.when(pair >= 0)
        def _():
            block_slot_ref[pair] = k

    for m in range(NBLK):
        for n in range(NBLK):
            rows, cols = pl.ds(m * B, B), pl.ds(n * B, B)
            occ = greens_ref[0, rows, cols].astype(jnp.float32)
            occ = jnp.where(mask_ref[m * NBLK + n] > 0, occ, 0.0)
            occ_t_ref[cols, rows] = occ.T.astype(jnp.bfloat16)
            virt = greens_ref[1, rows, cols].astype(jnp.float32)
            virt = jnp.where(mask_ref[NPAIR + m * NBLK + n] > 0, virt, 0.0)
            virt_ref[rows, cols] = virt.astype(jnp.bfloat16)

    def one(aux, carry):
        for m in range(NBLK):
            for n in range(NBLK):
                slot = block_slot_ref[m * NBLK + n]
                block = arrived_ref[jnp.maximum(slot, 0), aux].astype(jnp.float32)
                block = jnp.where(slot >= 0, block, 0.0)
                dense[m * B : (m + 1) * B, n * B : (n + 1) * B] = block.astype(jnp.bfloat16)
        half = jnp.dot(
            occ_t_ref[...], dense[...], preferred_element_type=jnp.float32
        ).astype(jnp.bfloat16)
        full = jnp.dot(half, virt_ref[...], preferred_element_type=jnp.float32)
        for m in range(NBLK):
            for sub in range(SUB):
                row = m * B + sub * NCHIP
                for n in range(NBLK):
                    scratch[(m * NBLK + n) * SUB + sub, pl.ds(aux, NCHIP, stride=AUX), :] = full[
                        row : row + NCHIP, n * B : (n + 1) * B
                    ]
        return carry

    lax.fori_loop(0, AUX, one, 0)
    for k in range(NPAIR * SUB):
        out_ref[:, k * B : (k + 1) * B] = scratch[k].astype(jnp.bfloat16)


def contracted_slices(block_pairs, mask, arrived, greens):
    return pl.pallas_call(
        contract_kernel,
        out_shape=jax.ShapeDtypeStruct((ROWS, NPAIR * SPAN), jnp.bfloat16),
        grid_spec=pltpu.PrefetchScalarGridSpec(
            num_scalar_prefetch=2,
            grid=(),
            in_specs=[VMEM] * 2,
            out_specs=VMEM,
            scratch_shapes=[
                pltpu.VMEM((NPAIR * SUB, ROWS, B), jnp.float32),
                pltpu.VMEM((NBAS, NBAS), jnp.bfloat16),
                pltpu.VMEM((NBAS, NBAS), jnp.bfloat16),
                pltpu.VMEM((NBAS, NBAS), jnp.bfloat16),
                pltpu.SMEM((NPAIR,), jnp.int32),
            ],
        ),
        compiler_params=pltpu.CompilerParams(vmem_limit_bytes=24 * MIB),
        name="contracted_slices",
    )(block_pairs, mask, arrived, greens)


def dense_kernel(block_pairs_ref, own_ref, other_ref, out_ref):
    core = lax.axis_index("c").astype(jnp.int32)

    def one(y, carry):
        rows = pl.ds(pl.multiple_of(y * AB, AB), AB)
        for ref, side in ((own_ref, core), (other_ref, 1 - core)):
            row = 2 * y + side
            cols = pl.ds(pl.multiple_of(row * AB, AB), AB)
            out_ref[:, cols] = jnp.zeros((NPAIR * SPAN, AB), jnp.bfloat16)

            def one_slot(k, place):
                pair = block_pairs_ref[row, k]

                @pl.when(pair >= 0)
                def _():
                    start = pl.multiple_of(pair * SPAN, SPAN)
                    from_ = pl.multiple_of(jnp.minimum(place, NNZ - 1) * SPAN, SPAN)
                    block = ref[rows, pl.ds(from_, SPAN)].astype(jnp.float32)
                    out_ref[pl.ds(start, SPAN), cols] = block.T.astype(jnp.bfloat16)

                return place + (pair >= 0).astype(jnp.int32)

            lax.fori_loop(0, N_COL, one_slot, jnp.int32(0))
        return carry

    lax.fori_loop(0, N_ROW // 2, one, 0)


def dense_named(block_pairs, own, other):
    return pl.pallas_call(
        dense_kernel,
        out_shape=jax.ShapeDtypeStruct((NPAIR * SPAN, N_ROW * AB), jnp.bfloat16),
        grid_spec=pltpu.PrefetchScalarGridSpec(
            num_scalar_prefetch=1,
            grid=(),
            in_specs=[VMEM] * 2,
            out_specs=VMEM,
        ),
        compiler_params=pltpu.CompilerParams(vmem_limit_bytes=18 * MIB),
        cost_estimate=pl.CostEstimate(flops=0, bytes_accessed=14 * MIB, transcendentals=0),
        name="dense_named",
    )(block_pairs, own, other)


STEPS = 4
PART = NPAIR * SPAN // STEPS
QCOLS = 256


def chi_kernel(image_hbm, dense_hbm, out_ref, image, dense, total, image_sem, dense_sem):
    copies = []
    for i in range(STEPS):
        part = pl.ds(i * PART, PART)
        copies.append(
            (
                pltpu.make_async_copy(image_hbm.at[:, part], image.at[:, part], image_sem.at[i]),
                pltpu.make_async_copy(dense_hbm.at[part], dense.at[part], dense_sem.at[i]),
            )
        )
    for pair in copies:
        for copy in pair:
            copy.start()
    for i in range(STEPS):
        for copy in copies[i]:
            copy.wait()
        for q in range(0, N_ROW * AB, QCOLS):
            term = jnp.dot(
                image[:, i * PART : (i + 1) * PART],
                dense[i * PART : (i + 1) * PART, q : q + QCOLS],
                preferred_element_type=jnp.float32,
            )
            if i == 0:
                total[:, q : q + QCOLS] = term
            elif i < STEPS - 1:
                total[:, q : q + QCOLS] += term
            else:
                out_ref[:, q : q + QCOLS] = (total[:, q : q + QCOLS] + term).astype(jnp.bfloat16)


def chi_partials(image, dense):
    return pl.pallas_call(
        chi_kernel,
        out_shape=jax.ShapeDtypeStruct((ROWS, N_ROW * AB), jnp.bfloat16),
        in_specs=[HBM, HBM],
        out_specs=VMEM,
        scratch_shapes=[
            pltpu.VMEM((ROWS, NPAIR * SPAN), jnp.bfloat16),
            pltpu.VMEM((NPAIR * SPAN, N_ROW * AB), jnp.bfloat16),
            pltpu.VMEM((ROWS, N_ROW * AB), jnp.float32),
            pltpu.SemaphoreType.DMA((STEPS,)),
            pltpu.SemaphoreType.DMA((STEPS,)),
        ],
        compiler_params=pltpu.CompilerParams(vmem_limit_bytes=58 * MIB),
        name="chi_partials",
    )(image, dense)


def on_device(x_slots, block_pairs, greens, green_mask, chi_mask):
    chips = ("y", "x", "z")
    arrived = lax.all_to_all(
        x_slots[0, 0].reshape(N_COL, AUX, B, B), ("x", "z"), 0, 0, tiled=True
    )
    own = named_slices(block_pairs, arrived)
    own = lax.all_to_all(
        own.reshape(NCHIP, AUX, NNZ * SPAN), chips, 0, 0, tiled=True
    ).reshape(ROWS, NNZ * SPAN)
    other = lax.ppermute(own, "c", [(0, 1), (1, 0)])
    image = contracted_slices(block_pairs, green_mask.reshape(2 * NPAIR), arrived, greens)
    image = lax.all_to_all(
        image.reshape(NCHIP, AUX, NPAIR * SPAN), chips, 0, 0, tiled=True
    ).reshape(ROWS, NPAIR * SPAN)
    dense = dense_named(block_pairs, own, other)
    part = chi_partials(image, dense)
    part = lax.all_to_all(part.reshape(NCHIP, AUX, N_ROW * AB), chips, 0, 0, tiled=True)
    part, chi_mask = lax.optimization_barrier((part, chi_mask))
    chi = jnp.sum(part.astype(jnp.float32), axis=0)
    return chi * jnp.repeat(chi_mask[0], AB).astype(jnp.float32)[None, :]


def solution(mesh):
    split = Mesh(mesh.devices.reshape(4, 2, 4, 4), ("y", "c", "x", "z"))
    row, col = ("y", "c"), ("x", "z")
    placed = (P(row, col, None, None, None), P(), P(), P(), P(row, None))
    return jax.shard_map(
        on_device,
        mesh=split,
        in_specs=placed,
        out_specs=P(row + col, None),
        check_vma=False,
    )
```

```python
import functools

import jax
import jax.numpy as jnp
from jax import lax
from jax.experimental import pallas as pl
from jax.experimental.pallas import tpu as pltpu
from jax.sharding import Mesh
from jax.sharding import PartitionSpec as P

B = 128
AB = 128
NBLK = 4
NPAIR = NBLK * NBLK
NBAS = NBLK * B
NNZ = 10
N_ROW = 8
N_COL = 16
AUX = AB // N_COL
NCHIP = 64
SUB = B // NCHIP
SPAN = SUB * B
ROWS = NCHIP * AUX
NAMED = NNZ * SPAN
WIDTH = NAMED + NPAIR * SPAN
MIB = 1024 * 1024
SMEM = pl.BlockSpec(memory_space=pltpu.SMEM)
VMEM = pl.BlockSpec(memory_space=pltpu.VMEM)


def slices_kernel(
    block_pairs_ref,
    mask_ref,
    arrived_ref,
    greens_ref,
    out_ref,
    pairs_ref,
    slot_of_ref,
    block_slot_ref,
    scratch,
    dense0,
    dense1,
    occ_t_ref,
    virt_ref,
):
    row = lax.axis_index(("y", "c")).astype(jnp.int32)
    for pair in range(NPAIR):
        block_slot_ref[pair] = -1
    place = jnp.int32(0)
    for k in range(N_COL):
        pair = block_pairs_ref[row, k]
        slot_of_ref[place] = k
        place = jnp.minimum(place + (pair >= 0).astype(jnp.int32), N_COL - 1)

        @pl.when(pair >= 0)
        def _():
            block_slot_ref[pair] = k

    for m in range(NBLK):
        for n in range(NBLK):
            rows, cols = pl.ds(m * B, B), pl.ds(n * B, B)
            occ = greens_ref[0, rows, cols].astype(jnp.float32)
            occ = jnp.where(mask_ref[0, m, n] > 0, occ, 0.0)
            occ_t_ref[cols, rows] = occ.T.astype(jnp.bfloat16)
            virt = greens_ref[1, rows, cols].astype(jnp.float32)
            virt = jnp.where(mask_ref[1, m, n] > 0, virt, 0.0)
            virt_ref[rows, cols] = virt.astype(jnp.bfloat16)

    def two(i, carry):
        for u, dense in enumerate((dense0, dense1)):
            aux = 2 * i + u
            for m in range(NBLK):
                for n in range(NBLK):
                    slot = block_slot_ref[m * NBLK + n]
                    block = arrived_ref[jnp.maximum(slot, 0), aux]
                    dense[m * B : (m + 1) * B, n * B : (n + 1) * B] = jnp.where(
                        slot >= 0, block, jnp.zeros_like(block)
                    )
            half = jnp.dot(
                occ_t_ref[...], dense[...], preferred_element_type=jnp.float32
            ).astype(jnp.bfloat16)
            for j in range(NNZ):
                block = arrived_ref[slot_of_ref[j], aux].astype(jnp.float32)
                for sub in range(SUB):
                    scratch[j * SUB + sub, pl.ds(aux, NCHIP, stride=AUX), :] = block[
                        sub * NCHIP : (sub + 1) * NCHIP
                    ]
            full = jnp.dot(half, virt_ref[...], preferred_element_type=jnp.float32)
            for m in range(NBLK):
                for sub in range(SUB):
                    at = m * B + sub * NCHIP
                    for n in range(NBLK):
                        k = (NNZ + m * NBLK + n) * SUB + sub
                        scratch[k, pl.ds(aux, NCHIP, stride=AUX), :] = full[
                            at : at + NCHIP, n * B : (n + 1) * B
                        ]
        return carry

    for i in range(AUX // 2):
        two(i, 0)

    def one_row(row, carry):
        def one_slot(k, place):
            pair = block_pairs_ref[row, k]
            pairs_ref[row, place] = jnp.maximum(pair, 0)
            return jnp.minimum(place + (pair >= 0).astype(jnp.int32), N_COL - 1)

        lax.fori_loop(0, N_COL, one_slot, jnp.int32(0))
        return carry

    lax.fori_loop(0, N_ROW, one_row, 0)
    for k in range((NNZ + NPAIR) * SUB):
        out_ref[:, k * B : (k + 1) * B] = scratch[k].astype(jnp.bfloat16)


def slices(block_pairs, mask, arrived, greens):
    return pl.pallas_call(
        slices_kernel,
        out_shape=(
            jax.ShapeDtypeStruct((ROWS, WIDTH), jnp.bfloat16),
            jax.ShapeDtypeStruct((N_ROW, N_COL), jnp.int32),
        ),
        grid_spec=pltpu.PrefetchScalarGridSpec(
            num_scalar_prefetch=2,
            grid=(),
            in_specs=[VMEM] * 2,
            out_specs=(VMEM, SMEM),
            scratch_shapes=[
                pltpu.SMEM((N_COL,), jnp.int32),
                pltpu.SMEM((NPAIR,), jnp.int32),
                pltpu.VMEM(((NNZ + NPAIR) * SUB, ROWS, B), jnp.float32),
                pltpu.VMEM((NBAS, NBAS), jnp.bfloat16),
                pltpu.VMEM((NBAS, NBAS), jnp.bfloat16),
                pltpu.VMEM((NBAS, NBAS), jnp.bfloat16),
                pltpu.VMEM((NBAS, NBAS), jnp.bfloat16),
            ],
        ),
        compiler_params=pltpu.CompilerParams(vmem_limit_bytes=36 * MIB),
        name="slices",
    )(block_pairs, mask, arrived, greens)


def chi_kernel(side_of, pairs_ref, received_ref, named_ref, *refs):
    out_ref, dense0, dense1 = refs[-3:]
    side = side_of(lax.axis_index("c").astype(jnp.int32))
    for h, dense in enumerate((dense0, dense1)):
        dense[...] = jnp.zeros((2 * AB, NPAIR * SPAN), jnp.bfloat16)
        for v in range(2):
            y = 2 * h + v
            for j in range(NNZ):
                start = pl.multiple_of(pairs_ref[2 * y + side, j] * SPAN, SPAN)
                dense[v * AB : (v + 1) * AB, pl.ds(start, SPAN)] = named_ref[
                    y * AB : (y + 1) * AB, j * SPAN : (j + 1) * SPAN
                ]
        part = lax.dot_general(
            received_ref[:, NAMED:],
            dense[...],
            (((1,), (1,)), ((), ())),
            preferred_element_type=jnp.float32,
        ).astype(jnp.bfloat16)
        for v in range(2):
            row = 2 * (2 * h + v) + side
            out_ref[:, pl.ds(pl.multiple_of(row * AB, AB), AB)] = part[:, v * AB : (v + 1) * AB]


def chi_half(name, side_of, pairs, received, named, *rest):
    return pl.pallas_call(
        functools.partial(chi_kernel, side_of),
        out_shape=jax.ShapeDtypeStruct((ROWS, N_ROW * AB), jnp.bfloat16),
        grid_spec=pltpu.PrefetchScalarGridSpec(
            num_scalar_prefetch=1,
            grid=(),
            in_specs=[VMEM] * (2 + len(rest)),
            out_specs=VMEM,
            scratch_shapes=[pltpu.VMEM((2 * AB, NPAIR * SPAN), jnp.bfloat16)] * 2,
        ),
        input_output_aliases={3: 0} if rest else {},
        cost_estimate=pl.CostEstimate(
            flops=ROWS * N_ROW * AB * NPAIR * SPAN, bytes_accessed=8 * MIB, transcendentals=0
        ),
        compiler_params=pltpu.CompilerParams(vmem_limit_bytes=16 * MIB),
        name=name,
    )(pairs, received, named, *rest)


def on_device(x_slots, block_pairs, greens, green_mask, chi_mask):
    chips = ("y", "x", "z")
    arrived = lax.all_to_all(
        x_slots[0, 0].reshape(N_COL, AUX, B, B), ("x", "z"), 0, 0, tiled=True
    )
    sent, pairs = slices(block_pairs, green_mask, arrived, greens)
    received = lax.all_to_all(sent.reshape(NCHIP, AUX, WIDTH), chips, 0, 0, tiled=True)
    received = received.reshape(ROWS, WIDTH)
    own = received[:, :NAMED]
    other = lax.ppermute(own, "c", [(0, 1), (1, 0)])
    part = chi_half("chi_own", lambda core: core, pairs, received, own)
    part = chi_half("chi_other", lambda core: 1 - core, pairs, received, other, part)
    part = lax.all_to_all(part.reshape(NCHIP, AUX, N_ROW * AB), chips, 0, 0, tiled=True)
    part, chi_mask = lax.optimization_barrier((part, chi_mask))
    chi = jnp.sum(part.astype(jnp.float32), axis=0)
    return chi * jnp.repeat(chi_mask[0], AB).astype(jnp.float32)[None, :]


def solution(mesh):
    split = Mesh(mesh.devices.reshape(4, 2, 4, 4), ("y", "c", "x", "z"))
    row, col = ("y", "c"), ("x", "z")
    placed = (P(row, col, None, None, None), P(), P(), P(), P(row, None))
    return jax.shard_map(
        on_device,
        mesh=split,
        in_specs=placed,
        out_specs=P(row + col, None),
        check_vma=False,
    )
```

```python
import jax
import jax.numpy as jnp
from jax import lax
from jax.experimental import pallas as pl
from jax.experimental.pallas import tpu as pltpu
from jax.sharding import Mesh
from jax.sharding import PartitionSpec as P

B = 128
AB = 128
NBLK = 4
NPAIR = NBLK * NBLK
NBAS = NBLK * B
NNZ = 10
N_ROW = 8
N_COL = 16
AUX = AB // N_COL
NCHIP = 64
SUB = B // NCHIP
SPAN = SUB * B
ROWS = NCHIP * AUX
NAMED = NNZ * SPAN
WIDTH = NAMED + NPAIR * SPAN
MIB = 1024 * 1024
SMEM = pl.BlockSpec(memory_space=pltpu.SMEM)
VMEM = pl.BlockSpec(memory_space=pltpu.VMEM)


def slices_kernel(
    block_pairs_ref,
    mask_ref,
    arrived_ref,
    greens_ref,
    out_ref,
    slot_of_ref,
    block_slot_ref,
    scratch,
    half_scratch,
    dense0,
    dense1,
    occ_t_ref,
    virt_ref,
):
    row = lax.axis_index(("y", "c")).astype(jnp.int32)
    for pair in range(NPAIR):
        block_slot_ref[pair] = -1
    place = jnp.int32(0)
    for k in range(N_COL):
        pair = block_pairs_ref[row, k]
        slot_of_ref[place] = k
        place = jnp.minimum(place + (pair >= 0).astype(jnp.int32), N_COL - 1)

        @pl.when(pair >= 0)
        def _():
            block_slot_ref[pair] = k

    for m in range(NBLK):
        for n in range(NBLK):
            rows, cols = pl.ds(m * B, B), pl.ds(n * B, B)
            occ = greens_ref[0, rows, cols].astype(jnp.float32)
            occ = jnp.where(mask_ref[0, m, n] > 0, occ, 0.0)
            occ_t_ref[cols, rows] = occ.T.astype(jnp.bfloat16)
            virt = greens_ref[1, rows, cols].astype(jnp.float32)
            virt = jnp.where(mask_ref[1, m, n] > 0, virt, 0.0)
            virt_ref[rows, cols] = virt.astype(jnp.bfloat16)

    def named_rows(aux):
        for j in range(NNZ):
            block = arrived_ref[slot_of_ref[j], aux].astype(jnp.float32)
            for sub in range(SUB):
                scratch[j * SUB + sub, pl.ds(aux, NCHIP, stride=AUX), :] = block[
                    sub * NCHIP : (sub + 1) * NCHIP
                ]

    for aux in range(AUX):
        dense = dense0 if aux % 2 == 0 else dense1
        for m in range(NBLK):
            for n in range(NBLK):
                slot = block_slot_ref[m * NBLK + n]
                block = arrived_ref[jnp.maximum(slot, 0), aux]
                dense[m * B : (m + 1) * B, n * B : (n + 1) * B] = jnp.where(
                    slot >= 0, block, jnp.zeros_like(block)
                )
        half = jnp.dot(occ_t_ref[...], dense[...], preferred_element_type=jnp.float32)
        named_rows(aux)
        for m in range(NBLK):
            for sub in range(SUB):
                at = m * B + sub * NCHIP
                for n in range(NBLK):
                    half_scratch[
                        (m * SUB + sub) * NBLK + n, pl.ds(aux, NCHIP, stride=AUX), :
                    ] = half[at : at + NCHIP, n * B : (n + 1) * B]
    for m in range(NBLK):
        for sub in range(SUB):
            at = (m * SUB + sub) * NBLK
            half = jnp.concatenate(
                [half_scratch[at + n].astype(jnp.bfloat16) for n in range(NBLK)], axis=1
            )
            full = jnp.dot(half, virt_ref[...], preferred_element_type=jnp.float32)
            for n in range(NBLK):
                k = (NNZ + m * NBLK + n) * SUB + sub
                out_ref[:, k * B : (k + 1) * B] = full[:, n * B : (n + 1) * B].astype(
                    jnp.bfloat16
                )
            for k in range(m * SUB + sub, NNZ * SUB, NBLK * SUB):
                out_ref[:, k * B : (k + 1) * B] = scratch[k].astype(jnp.bfloat16)


def slices(block_pairs, mask, arrived, greens):
    return pl.pallas_call(
        slices_kernel,
        out_shape=jax.ShapeDtypeStruct((ROWS, WIDTH), jnp.bfloat16),
        grid_spec=pltpu.PrefetchScalarGridSpec(
            num_scalar_prefetch=2,
            grid=(),
            in_specs=[VMEM] * 2,
            out_specs=VMEM,
            scratch_shapes=[
                pltpu.SMEM((N_COL,), jnp.int32),
                pltpu.SMEM((NPAIR,), jnp.int32),
                pltpu.VMEM((NNZ * SUB, ROWS, B), jnp.float32),
                pltpu.VMEM((NBLK * SUB * NBLK, ROWS, B), jnp.float32),
                pltpu.VMEM((NBAS, NBAS), jnp.bfloat16),
                pltpu.VMEM((NBAS, NBAS), jnp.bfloat16),
                pltpu.VMEM((NBAS, NBAS), jnp.bfloat16),
                pltpu.VMEM((NBAS, NBAS), jnp.bfloat16),
            ],
        ),
        compiler_params=pltpu.CompilerParams(vmem_limit_bytes=36 * MIB),
        name="slices",
    )(block_pairs, mask, arrived, greens)


def chi_rows(side, pairs_ref, received_ref, named_ref, out_ref, dense_refs):
    for h, dense in enumerate(dense_refs):
        dense[...] = jnp.zeros((2 * AB, NPAIR * SPAN), jnp.bfloat16)
        for v in range(2):
            y = 2 * h + v
            for j in range(NNZ):
                start = pl.multiple_of(pairs_ref[2 * y + side, j] * SPAN, SPAN)
                dense[v * AB : (v + 1) * AB, pl.ds(start, SPAN)] = named_ref[
                    y * AB : (y + 1) * AB, j * SPAN : (j + 1) * SPAN
                ]
        part = lax.dot_general(
            received_ref[:, NAMED:],
            dense[...],
            (((1,), (1,)), ((), ())),
            preferred_element_type=jnp.float32,
        ).astype(jnp.bfloat16)
        for v in range(2):
            row = 2 * (2 * h + v) + side
            out_ref[:, pl.ds(pl.multiple_of(row * AB, AB), AB)] = part[:, v * AB : (v + 1) * AB]


def own_kernel(block_pairs_ref, received_ref, out_ref, pairs_ref, *dense_refs):
    for row in range(N_ROW):
        place = jnp.int32(0)
        for k in range(N_COL):
            pair = block_pairs_ref[row, k]
            pairs_ref[row, place] = jnp.maximum(pair, 0)
            place = jnp.minimum(place + (pair >= 0).astype(jnp.int32), N_COL - 1)
    core = lax.axis_index("c").astype(jnp.int32)
    chi_rows(core, pairs_ref, received_ref, received_ref, out_ref, dense_refs)


def other_kernel(pairs_ref, received_ref, named_ref, part_ref, out_ref, *dense_refs):
    del part_ref
    core = lax.axis_index("c").astype(jnp.int32)
    chi_rows(1 - core, pairs_ref, received_ref, named_ref, out_ref, dense_refs)


def chi_half(kernel, name, *operands):
    first = len(operands) == 2
    part = jax.ShapeDtypeStruct((ROWS, N_ROW * AB), jnp.bfloat16)
    table = jax.ShapeDtypeStruct((N_ROW, N_COL), jnp.int32)
    return pl.pallas_call(
        kernel,
        out_shape=(part, table) if first else part,
        grid_spec=pltpu.PrefetchScalarGridSpec(
            num_scalar_prefetch=1,
            grid=(),
            in_specs=[VMEM] * (len(operands) - 1),
            out_specs=(VMEM, SMEM) if first else VMEM,
            scratch_shapes=[pltpu.VMEM((2 * AB, NPAIR * SPAN), jnp.bfloat16)] * 2,
        ),
        input_output_aliases={} if first else {3: 0},
        cost_estimate=pl.CostEstimate(
            flops=ROWS * N_ROW * AB * NPAIR * SPAN, bytes_accessed=8 * MIB, transcendentals=0
        ),
        compiler_params=pltpu.CompilerParams(vmem_limit_bytes=16 * MIB),
        name=name,
    )(*operands)


def on_device(x_slots, block_pairs, greens, green_mask, chi_mask):
    chips = ("y", "x", "z")
    arrived = lax.all_to_all(
        x_slots[0, 0].reshape(N_COL, AUX, B, B), ("x", "z"), 0, 0, tiled=True
    )
    sent = slices(block_pairs, green_mask, arrived, greens)
    received = lax.all_to_all(sent.reshape(NCHIP, AUX, WIDTH), chips, 0, 0, tiled=True)
    received = received.reshape(ROWS, WIDTH)
    own = received[:, :NAMED]
    other = lax.ppermute(own, "c", [(0, 1), (1, 0)])
    part, pairs = chi_half(own_kernel, "chi_own", block_pairs, received)
    part = chi_half(other_kernel, "chi_other", pairs, received, other, part)
    part = lax.all_to_all(part.reshape(NCHIP, AUX, N_ROW * AB), chips, 0, 0, tiled=True)
    part, chi_mask = lax.optimization_barrier((part, chi_mask))
    chi = jnp.sum(part.astype(jnp.float32), axis=0)
    return chi * jnp.repeat(chi_mask[0], AB).astype(jnp.float32)[None, :]


def solution(mesh):
    split = Mesh(mesh.devices.reshape(4, 2, 4, 4), ("y", "c", "x", "z"))
    row, col = ("y", "c"), ("x", "z")
    placed = (P(row, col, None, None, None), P(), P(), P(), P(row, None))
    return jax.shard_map(
        on_device,
        mesh=split,
        in_specs=placed,
        out_specs=P(row + col, None),
        check_vma=False,
    )
```

```python
import jax
import jax.numpy as jnp
from jax import lax
from jax.experimental import pallas as pl
from jax.experimental.pallas import tpu as pltpu
from jax.sharding import Mesh
from jax.sharding import PartitionSpec as P

B = 128
AB = 128
NBLK = 4
NPAIR = NBLK * NBLK
NBAS = NBLK * B
NNZ = 10
N_ROW = 8
N_COL = 16
AUX = AB // N_COL
NCHIP = 64
SUB = B // NCHIP
SPAN = SUB * B
ROWS = NCHIP * AUX
NAMED = NNZ * SPAN
WIDTH = NAMED + NPAIR * SPAN
MIB = 1024 * 1024
SMEM = pl.BlockSpec(memory_space=pltpu.SMEM)
VMEM = pl.BlockSpec(memory_space=pltpu.VMEM)


def slices_kernel(
    block_pairs_ref,
    mask_ref,
    arrived_ref,
    greens_ref,
    out_ref,
    slot_of_ref,
    block_slot_ref,
    scratch,
    half_scratch,
    occ_t_ref,
    virt_ref,
):
    row = lax.axis_index(("y", "c")).astype(jnp.int32)
    for pair in range(NPAIR):
        block_slot_ref[pair] = -1
    place = jnp.int32(0)
    for k in range(N_COL):
        pair = block_pairs_ref[row, k]
        slot_of_ref[place] = k
        place = jnp.minimum(place + (pair >= 0).astype(jnp.int32), N_COL - 1)

        @pl.when(pair >= 0)
        def _():
            block_slot_ref[pair] = k

    for m in range(NBLK):
        for n in range(NBLK):
            rows, cols = pl.ds(m * B, B), pl.ds(n * B, B)
            occ = greens_ref[0, rows, cols].astype(jnp.float32)
            occ = jnp.where(mask_ref[0, m, n] > 0, occ, 0.0)
            occ_t_ref[cols, rows] = occ.T.astype(jnp.bfloat16)
            virt = greens_ref[1, rows, cols].astype(jnp.float32)
            virt = jnp.where(mask_ref[1, m, n] > 0, virt, 0.0)
            virt_ref[rows, cols] = virt.astype(jnp.bfloat16)

    def named_rows(aux):
        for j in range(NNZ):
            block = arrived_ref[slot_of_ref[j], aux].astype(jnp.float32)
            for sub in range(SUB):
                scratch[j * SUB + sub, pl.ds(aux, NCHIP, stride=AUX), :] = block[
                    sub * NCHIP : (sub + 1) * NCHIP
                ]

    for aux in range(AUX):
        block_rows = []
        for m in range(NBLK):
            blocks = []
            for n in range(NBLK):
                slot = block_slot_ref[m * NBLK + n]
                block = arrived_ref[jnp.maximum(slot, 0), aux]
                blocks.append(jnp.where(slot >= 0, block, jnp.zeros_like(block)))
            block_rows.append(jnp.concatenate(blocks, axis=1))
        half = jnp.dot(
            occ_t_ref[...],
            jnp.concatenate(block_rows, axis=0),
            preferred_element_type=jnp.float32,
        )
        named_rows(aux)
        for m in range(NBLK):
            for sub in range(SUB):
                at = m * B + sub * NCHIP
                for n in range(NBLK):
                    half_scratch[
                        (m * SUB + sub) * NBLK + n, pl.ds(aux, NCHIP, stride=AUX), :
                    ] = half[at : at + NCHIP, n * B : (n + 1) * B]
    for m in range(NBLK):
        for sub in range(SUB):
            at = (m * SUB + sub) * NBLK
            half = jnp.concatenate(
                [half_scratch[at + n].astype(jnp.bfloat16) for n in range(NBLK)], axis=1
            )
            full = jnp.dot(half, virt_ref[...], preferred_element_type=jnp.float32)
            for n in range(NBLK):
                k = (NNZ + m * NBLK + n) * SUB + sub
                out_ref[:, k * B : (k + 1) * B] = full[:, n * B : (n + 1) * B].astype(
                    jnp.bfloat16
                )
            for k in range(m * SUB + sub, NNZ * SUB, NBLK * SUB):
                out_ref[:, k * B : (k + 1) * B] = scratch[k].astype(jnp.bfloat16)


def slices(block_pairs, mask, arrived, greens):
    return pl.pallas_call(
        slices_kernel,
        out_shape=jax.ShapeDtypeStruct((ROWS, WIDTH), jnp.bfloat16),
        grid_spec=pltpu.PrefetchScalarGridSpec(
            num_scalar_prefetch=2,
            grid=(),
            in_specs=[VMEM] * 2,
            out_specs=VMEM,
            scratch_shapes=[
                pltpu.SMEM((N_COL,), jnp.int32),
                pltpu.SMEM((NPAIR,), jnp.int32),
                pltpu.VMEM((NNZ * SUB, ROWS, B), jnp.float32),
                pltpu.VMEM((NBLK * SUB * NBLK, ROWS, B), jnp.float32),
                pltpu.VMEM((NBAS, NBAS), jnp.bfloat16),
                pltpu.VMEM((NBAS, NBAS), jnp.bfloat16),
            ],
        ),
        compiler_params=pltpu.CompilerParams(vmem_limit_bytes=36 * MIB),
        name="slices",
    )(block_pairs, mask, arrived, greens)


def chi_rows(side, pairs_ref, received_ref, named_ref, out_ref, dense_refs):
    for h, dense in enumerate(dense_refs):
        dense[...] = jnp.zeros((2 * AB, NPAIR * SPAN), jnp.bfloat16)
        for v in range(2):
            y = 2 * h + v
            for j in range(NNZ):
                start = pl.multiple_of(pairs_ref[2 * y + side, j] * SPAN, SPAN)
                dense[v * AB : (v + 1) * AB, pl.ds(start, SPAN)] = named_ref[
                    y * AB : (y + 1) * AB, j * SPAN : (j + 1) * SPAN
                ]
        part = lax.dot_general(
            received_ref[:, NAMED:],
            dense[...],
            (((1,), (1,)), ((), ())),
            preferred_element_type=jnp.float32,
        ).astype(jnp.bfloat16)
        for v in range(2):
            row = 2 * (2 * h + v) + side
            out_ref[:, pl.ds(pl.multiple_of(row * AB, AB), AB)] = part[:, v * AB : (v + 1) * AB]


def own_kernel(block_pairs_ref, received_ref, out_ref, pairs_ref, *dense_refs):
    for row in range(N_ROW):
        place = jnp.int32(0)
        for k in range(N_COL):
            pair = block_pairs_ref[row, k]
            pairs_ref[row, place] = jnp.maximum(pair, 0)
            place = jnp.minimum(place + (pair >= 0).astype(jnp.int32), N_COL - 1)
    core = lax.axis_index("c").astype(jnp.int32)
    chi_rows(core, pairs_ref, received_ref, received_ref, out_ref, dense_refs)


def other_kernel(pairs_ref, received_ref, named_ref, part_ref, out_ref, *dense_refs):
    del part_ref
    core = lax.axis_index("c").astype(jnp.int32)
    chi_rows(1 - core, pairs_ref, received_ref, named_ref, out_ref, dense_refs)


def chi_half(kernel, name, *operands):
    first = len(operands) == 2
    part = jax.ShapeDtypeStruct((ROWS, N_ROW * AB), jnp.bfloat16)
    table = jax.ShapeDtypeStruct((N_ROW, N_COL), jnp.int32)
    return pl.pallas_call(
        kernel,
        out_shape=(part, table) if first else part,
        grid_spec=pltpu.PrefetchScalarGridSpec(
            num_scalar_prefetch=1,
            grid=(),
            in_specs=[VMEM] * (len(operands) - 1),
            out_specs=(VMEM, SMEM) if first else VMEM,
            scratch_shapes=[pltpu.VMEM((2 * AB, NPAIR * SPAN), jnp.bfloat16)] * 2,
        ),
        input_output_aliases={} if first else {3: 0},
        cost_estimate=pl.CostEstimate(
            flops=ROWS * N_ROW * AB * NPAIR * SPAN, bytes_accessed=8 * MIB, transcendentals=0
        ),
        compiler_params=pltpu.CompilerParams(vmem_limit_bytes=16 * MIB),
        name=name,
    )(*operands)


def on_device(x_slots, block_pairs, greens, green_mask, chi_mask):
    chips = ("y", "x", "z")
    arrived = lax.all_to_all(
        x_slots[0, 0].reshape(N_COL, AUX, B, B), ("x", "z"), 0, 0, tiled=True
    )
    sent = slices(block_pairs, green_mask, arrived, greens)
    received = lax.all_to_all(sent.reshape(NCHIP, AUX, WIDTH), chips, 0, 0, tiled=True)
    received = received.reshape(ROWS, WIDTH)
    own = received[:, :NAMED]
    other = lax.ppermute(own, "c", [(0, 1), (1, 0)])
    part, pairs = chi_half(own_kernel, "chi_own", block_pairs, received)
    part = chi_half(other_kernel, "chi_other", pairs, received, other, part)
    part = lax.all_to_all(part.reshape(NCHIP, AUX, N_ROW * AB), chips, 0, 0, tiled=True)
    part, chi_mask = lax.optimization_barrier((part, chi_mask))
    chi = jnp.sum(part.astype(jnp.float32), axis=0)
    return chi * jnp.repeat(chi_mask[0], AB).astype(jnp.float32)[None, :]


def solution(mesh):
    split = Mesh(mesh.devices.reshape(4, 2, 4, 4), ("y", "c", "x", "z"))
    row, col = ("y", "c"), ("x", "z")
    placed = (P(row, col, None, None, None), P(), P(), P(), P(row, None))
    return jax.shard_map(
        on_device,
        mesh=split,
        in_specs=placed,
        out_specs=P(row + col, None),
        check_vma=False,
    )
```

```python
import jax
import jax.numpy as jnp
from jax import lax
from jax.experimental import pallas as pl
from jax.experimental.pallas import tpu as pltpu
from jax.sharding import Mesh
from jax.sharding import PartitionSpec as P

B = 128
AB = 128
NBLK = 4
NPAIR = NBLK * NBLK
NBAS = NBLK * B
NNZ = 10
N_ROW = 8
N_COL = 16
AUX = AB // N_COL
NCHIP = 64
SUB = B // NCHIP
SPAN = SUB * B
ROWS = NCHIP * AUX
NAMED = NNZ * SPAN
WIDTH = NAMED + NPAIR * SPAN
MIB = 1024 * 1024
SMEM = pl.BlockSpec(memory_space=pltpu.SMEM)
VMEM = pl.BlockSpec(memory_space=pltpu.VMEM)


def slices_kernel(
    block_pairs_ref,
    mask_ref,
    arrived_ref,
    greens_ref,
    out_ref,
    slot_of_ref,
    block_slot_ref,
    scratch,
    half_scratch,
    occ_t_ref,
    virt_ref,
):
    row = lax.axis_index(("y", "c")).astype(jnp.int32)
    for pair in range(NPAIR):
        block_slot_ref[pair] = -1
    place = jnp.int32(0)
    for k in range(N_COL):
        pair = block_pairs_ref[row, k]
        slot_of_ref[place] = k
        place = jnp.minimum(place + (pair >= 0).astype(jnp.int32), N_COL - 1)

        @pl.when(pair >= 0)
        def _():
            block_slot_ref[pair] = k

    for m in range(NBLK):
        for n in range(NBLK):
            rows, cols = pl.ds(m * B, B), pl.ds(n * B, B)
            occ = greens_ref[0, rows, cols].astype(jnp.float32)
            occ = jnp.where(mask_ref[0, m, n] > 0, occ, 0.0)
            occ_t_ref[cols, rows] = occ.T.astype(jnp.bfloat16)
            virt = greens_ref[1, rows, cols].astype(jnp.float32)
            virt = jnp.where(mask_ref[1, m, n] > 0, virt, 0.0)
            virt_ref[rows, cols] = virt.astype(jnp.bfloat16)

    def named_rows(aux):
        for j in range(NNZ):
            block = arrived_ref[slot_of_ref[j], aux].astype(jnp.float32)
            for sub in range(SUB):
                scratch[j * SUB + sub, pl.ds(aux, NCHIP, stride=AUX), :] = block[
                    sub * NCHIP : (sub + 1) * NCHIP
                ]

    for aux in range(AUX):
        block_rows = []
        for m in range(NBLK):
            blocks = []
            for n in range(NBLK):
                slot = block_slot_ref[m * NBLK + n]
                block = arrived_ref[jnp.maximum(slot, 0), aux]
                blocks.append(jnp.where(slot >= 0, block, jnp.zeros_like(block)))
            block_rows.append(jnp.concatenate(blocks, axis=1))
        half = jnp.dot(
            occ_t_ref[...],
            jnp.concatenate(block_rows, axis=0),
            preferred_element_type=jnp.float32,
        )
        named_rows(aux)
        for m in range(NBLK):
            for sub in range(SUB):
                at = m * B + sub * NCHIP
                for n in range(NBLK):
                    half_scratch[
                        (m * SUB + sub) * NBLK + n, pl.ds(aux, NCHIP, stride=AUX), :
                    ] = half[at : at + NCHIP, n * B : (n + 1) * B]
    for m in range(NBLK):
        for sub in range(SUB):
            at = (m * SUB + sub) * NBLK
            half = jnp.concatenate(
                [half_scratch[at + n].astype(jnp.bfloat16) for n in range(NBLK)], axis=1
            )
            full = jnp.dot(half, virt_ref[...], preferred_element_type=jnp.float32)
            for n in range(NBLK):
                k = (NNZ + m * NBLK + n) * SUB + sub
                out_ref[:, k * B : (k + 1) * B] = full[:, n * B : (n + 1) * B].astype(
                    jnp.bfloat16
                )
            for k in range(m * SUB + sub, NNZ * SUB, NBLK * SUB):
                out_ref[:, k * B : (k + 1) * B] = scratch[k].astype(jnp.bfloat16)


def slices(block_pairs, mask, arrived, greens):
    return pl.pallas_call(
        slices_kernel,
        out_shape=jax.ShapeDtypeStruct((ROWS, WIDTH), jnp.bfloat16),
        grid_spec=pltpu.PrefetchScalarGridSpec(
            num_scalar_prefetch=2,
            grid=(),
            in_specs=[VMEM] * 2,
            out_specs=VMEM,
            scratch_shapes=[
                pltpu.SMEM((N_COL,), jnp.int32),
                pltpu.SMEM((NPAIR,), jnp.int32),
                pltpu.VMEM((NNZ * SUB, ROWS, B), jnp.float32),
                pltpu.VMEM((NBLK * SUB * NBLK, ROWS, B), jnp.float32),
                pltpu.VMEM((NBAS, NBAS), jnp.bfloat16),
                pltpu.VMEM((NBAS, NBAS), jnp.bfloat16),
            ],
        ),
        compiler_params=pltpu.CompilerParams(vmem_limit_bytes=36 * MIB),
        name="slices",
    )(block_pairs, mask, arrived, greens)


def chi_rows(side, pairs_ref, received_ref, named_ref, out_ref, dense_refs, blank):
    for h, dense in enumerate(dense_refs):
        if blank:
            dense[...] = jnp.zeros((2 * AB, NPAIR * SPAN), jnp.bfloat16)
        for v in range(2):
            y = 2 * h + v
            for j in range(NNZ):
                start = pl.multiple_of(pairs_ref[2 * y + side, j] * SPAN, SPAN)
                dense[v * AB : (v + 1) * AB, pl.ds(start, SPAN)] = named_ref[
                    y * AB : (y + 1) * AB, j * SPAN : (j + 1) * SPAN
                ]
        part = lax.dot_general(
            received_ref[:, NAMED:],
            dense[...],
            (((1,), (1,)), ((), ())),
            preferred_element_type=jnp.float32,
        ).astype(jnp.bfloat16)
        for v in range(2):
            row = 2 * (2 * h + v) + side
            out_ref[:, pl.ds(pl.multiple_of(row * AB, AB), AB)] = part[:, v * AB : (v + 1) * AB]


def own_kernel(block_pairs_ref, received_ref, out_ref, pairs_ref, zero0_ref, zero1_ref, *dense_refs):
    zero0_ref[...] = jnp.zeros((2 * AB, NPAIR * SPAN), jnp.bfloat16)
    zero1_ref[...] = jnp.zeros((2 * AB, NPAIR * SPAN), jnp.bfloat16)
    for row in range(N_ROW):
        place = jnp.int32(0)
        for k in range(N_COL):
            pair = block_pairs_ref[row, k]
            pairs_ref[row, place] = jnp.maximum(pair, 0)
            place = jnp.minimum(place + (pair >= 0).astype(jnp.int32), N_COL - 1)
    core = lax.axis_index("c").astype(jnp.int32)
    chi_rows(core, pairs_ref, received_ref, received_ref, out_ref, dense_refs, True)


def other_kernel(
    pairs_ref, received_ref, named_ref, part_ref, zero0_ref, zero1_ref, out_ref, *dense_refs
):
    del part_ref, zero0_ref, zero1_ref
    core = lax.axis_index("c").astype(jnp.int32)
    chi_rows(1 - core, pairs_ref, received_ref, named_ref, out_ref, dense_refs, False)


def chi_half(kernel, name, *operands):
    first = len(operands) == 2
    part = jax.ShapeDtypeStruct((ROWS, N_ROW * AB), jnp.bfloat16)
    table = jax.ShapeDtypeStruct((N_ROW, N_COL), jnp.int32)
    dense = [jax.ShapeDtypeStruct((2 * AB, NPAIR * SPAN), jnp.bfloat16)] * 2
    return pl.pallas_call(
        kernel,
        out_shape=(part, table, *dense) if first else (part, *dense),
        grid_spec=pltpu.PrefetchScalarGridSpec(
            num_scalar_prefetch=1,
            grid=(),
            in_specs=[VMEM] * (len(operands) - 1),
            out_specs=(VMEM, SMEM, VMEM, VMEM) if first else (VMEM,) * 3,
            scratch_shapes=[pltpu.VMEM((2 * AB, NPAIR * SPAN), jnp.bfloat16)] * (2 if first else 0),
        ),
        input_output_aliases={} if first else {3: 0, 4: 1, 5: 2},
        cost_estimate=pl.CostEstimate(
            flops=ROWS * N_ROW * AB * NPAIR * SPAN, bytes_accessed=8 * MIB, transcendentals=0
        ),
        compiler_params=pltpu.CompilerParams(vmem_limit_bytes=16 * MIB),
        name=name,
    )(*operands)


def on_device(x_slots, block_pairs, greens, green_mask, chi_mask):
    chips = ("y", "x", "z")
    arrived = lax.all_to_all(
        x_slots[0, 0].reshape(N_COL, AUX, B, B), ("x", "z"), 0, 0, tiled=True
    )
    sent = slices(block_pairs, green_mask, arrived, greens)
    received = lax.all_to_all(sent.reshape(NCHIP, AUX, WIDTH), chips, 0, 0, tiled=True)
    received = received.reshape(ROWS, WIDTH)
    own = received[:, :NAMED]
    other = lax.ppermute(own, "c", [(0, 1), (1, 0)])
    part, pairs, *zeros = chi_half(own_kernel, "chi_own", block_pairs, received)
    part = chi_half(other_kernel, "chi_other", pairs, received, other, part, *zeros)[0]
    part = lax.all_to_all(part.reshape(NCHIP, AUX, N_ROW * AB), chips, 0, 0, tiled=True)
    part, chi_mask = lax.optimization_barrier((part, chi_mask))
    chi = jnp.sum(part.astype(jnp.float32), axis=0)
    return chi * jnp.repeat(chi_mask[0], AB).astype(jnp.float32)[None, :]


def solution(mesh):
    split = Mesh(mesh.devices.reshape(4, 2, 4, 4), ("y", "c", "x", "z"))
    row, col = ("y", "c"), ("x", "z")
    placed = (P(row, col, None, None, None), P(), P(), P(), P(row, None))
    return jax.shard_map(
        on_device,
        mesh=split,
        in_specs=placed,
        out_specs=P(row + col, None),
        check_vma=False,
    )
```
